32 devices in a mesh: dp: 8 (over z, x), ctx: 4 (over y, core).
Axes of the slice: x: 2, y: 2, z: 4, core: 2. Of those that a mesh axis runs over, the one named last changes fastest.
Arguments:
- block_input: bfloat16 [8, 512, 1024], P('dp', 'ctx'), may hold values from -6 to 6
- segment_ids: int32 [8, 512], P('dp'), may hold values from 0 to 2, never falling along the last dimension, each value on 1 to 320 neighbouring positions
- ln1_gain: bfloat16 [1024], P('dp'), may hold values from 0.25 to 1.75
- ln1_bias: bfloat16 [1024], P('dp'), may hold values from -3 to 3
- qkv_weight: bfloat16 [1024, 3, 1024], P('dp', None, 'ctx'), may hold values from -3 to 3
- query_bias: bfloat16 [1024], P('dp'), may hold values from -3 to 3
- value_bias: bfloat16 [1024], P('dp'), may hold values from -1.1953125 to 1.1953125
- proj_weight: bfloat16 [1024, 1024], P('ctx', 'dp'), may hold values from -0.75 to 0.75
- proj_bias: bfloat16 [1024], P('dp'), may hold values from -3 to 3
- ln2_gain: bfloat16 [1024], P('dp'), may hold values from 0.25 to 1.75
- ln2_bias: bfloat16 [1024], P('dp'), may hold values from -3 to 3
- fc_weight: bfloat16 [1024, 4096], P('dp', 'ctx'), may hold values from -0.1875 to 0.1875
- fc_bias: bfloat16 [4096], P('dp'), may hold values from -3 to 3
- out_weight: bfloat16 [4096, 1024], P('ctx', 'dp'), may hold values from -0.09375 to 0.09375
- out_bias: bfloat16 [1024], P('dp'), may hold values from -3 to 3
- cotangent: bfloat16 [8, 512, 1024], P('dp', 'ctx'), may hold values from -6 to 6
Outputs:
- block_output: bfloat16 [8, 512, 1024], P('dp', 'ctx')
- input_grad: float32 [8, 512, 1024], P('dp', 'ctx')
- ln1_gain_grad: float32 [1024], P('dp')
- ln1_bias_grad: float32 [1024], P('dp')
- qkv_weight_grad: float32 [1024, 3, 1024], P('dp', None, 'ctx')
- query_bias_grad: float32 [1024], P('dp')
- value_bias_grad: float32 [1024], P('dp')
- proj_weight_grad: float32 [1024, 1024], P('ctx', 'dp')
- proj_bias_grad: float32 [1024], P('dp')
- ln2_gain_grad: float32 [1024], P('dp')
- ln2_bias_grad: float32 [1024], P('dp')
- fc_weight_grad: float32 [1024, 4096], P('dp', 'ctx')
- fc_bias_grad: float32 [4096], P('dp')
- out_weight_grad: float32 [4096, 1024], P('ctx', 'dp')
- out_bias_grad: float32 [1024], P('dp')
The draws below stay inside these ranges and needn't reach their ends.
Inputs may be any that keep to these rules, and one draw needn't show every extreme that they name: `segment_ids`: segment numbers never fall along a sequence.
All inputs are finite; a program needn't handle non-finite values.
Results may differ from the reference program's by a relative error of at most 0.019.
Values may be sent and summed in bfloat16 or wider, within the bound.
A program may use at most 128 MiB of HBM per device.

```python
import math
import jax
import jax.numpy as jnp
import numpy as np
from jax import lax

D = 1024
HEADS = 16
HD = 64
FF = 4096
SEQ_LEN = 512
SEQS = 8


def draw_qkv_weight(key, part):
    normal_base = jax.random.normal(jax.random.fold_in(key, 11), (D, 3 * D), jnp.float32)
    return (jnp.clip(normal_base, -6.0, 6.0) / math.sqrt(D)).reshape(D, 3, D).astype(jnp.bfloat16)


def spiked(result, key, source, target, shards_of, factor):
    owner, partner = [(jnp.arange(result.shape[position]) // (result.shape[position] // shards_of)).reshape([-1 if axis == position else 1 for axis in range(result.ndim)]) for position in (source, target)]
    chosen = jax.random.permutation(key, shards_of)[partner]
    strong = (owner == chosen) | (owner == (partner + shards_of // 2) % shards_of)
    return jnp.where(strong, factor * result, result)


def block_levels(stream_key, shape, pieces, smallest, high):
    loudness, own = 1.0, jax.random.fold_in(stream_key, 6)
    for axis_at, shards_of in pieces:
        draws = jnp.exp(jax.random.uniform(jax.random.fold_in(own, axis_at), (shards_of,), jnp.float32, smallest / len(pieces), high / len(pieces)))
        loudness = loudness * jnp.repeat(draws, shape[axis_at] // shards_of).reshape([-1 if axis == axis_at else 1 for axis in range(len(shape))])
    return loudness


def profile(count, total, reach, lean):
    portions = [(1 << 20) // math.isqrt(standing ** lean) + 1 for standing in range(2, count + 1)]
    rest, counts = total - reach - (count - 1), [1] * (count - 1)
    while rest > 0:
        free = [i for i in range(count - 1) if counts[i] < reach]
        pool, remaining = sum([portions[i] for i in free]), rest
        for i in free:
            extra = min(reach - counts[i], max(1, remaining * portions[i] // pool), rest)
            counts[i] = counts[i] + extra
            rest = rest - extra
    return np.array([reach] + counts)


def uneven_parts(rng, count, total, limit, skew):
    if count == 2:
        one = jax.random.randint(rng, (), max(1, total - limit), min(limit, total - 1) + 1)
        return jnp.stack([one, total - one])
    sizes = jnp.asarray(profile(count, total, limit, skew), jnp.int32)
    pairs = (count - 1) // 2
    source_of, sink = sizes[1:1 + 2 * pairs:2], sizes[2:2 + 2 * pairs:2]
    margin = jnp.minimum(source_of - 1, limit - sink)
    moved = jax.random.randint(jax.random.fold_in(rng, 1), (pairs,), 0, 1 << 20) % (margin + 1)
    sizes = sizes.at[1:1 + 2 * pairs:2].set(source_of - moved).at[2:2 + 2 * pairs:2].set(sink + moved)
    return sizes[jax.random.permutation(jax.random.fold_in(rng, 2), count)]


def noise(own_key, extent, deviation, bound, cuts=(), held_as=jnp.bfloat16):
    level = block_levels(own_key, extent, cuts, -0.22, 0.18) if cuts else 1.0
    drawn = jax.random.normal(own_key, extent, jnp.float32) * deviation * level
    return jnp.minimum(jnp.maximum(drawn, -bound), bound).astype(held_as)


def heavy_noise(own_key, extent, width, reach, cuts, heavy, kind=jnp.bfloat16):
    drawn = width * jax.random.normal(own_key, extent, jnp.float32)
    if cuts:
        drawn = drawn * block_levels(own_key, extent, cuts, -0.22, 0.18)
    return jnp.clip(spiked(drawn, jax.random.fold_in(own_key, 3), *heavy), -reach, reach).astype(kind)


def setup_inputs(seed: int = 0) -> dict:
    keys = jax.random.split(jax.random.key(seed), 17)
    return {
        "block_input": noise(keys[0], (SEQS, SEQ_LEN, D), 1.0, 6.0, ((0, 8), (1, 4))),
        "segment_ids": jax.vmap(lambda own: jnp.searchsorted(jnp.cumsum(uneven_parts(own, 3, SEQ_LEN, SEQ_LEN // 2 + SEQ_LEN // 8, 0)), jnp.arange(SEQ_LEN), side="right"))(jax.random.split(keys[1], SEQS)).reshape((SEQS, SEQ_LEN)).astype(jnp.int32),
        "ln1_gain": jnp.clip(1.0 + 0.15 * jax.random.normal(keys[2], (D,), jnp.float32), 0.25, 1.75).astype(jnp.bfloat16),
        "ln1_bias": noise(keys[3], (D,), 0.5, 3.0, ((0, 8),)),
        "qkv_weight": draw_qkv_weight(jax.random.fold_in(keys[16], 71), 0),
        "query_bias": noise(keys[5], (D,), 0.5, 3.0, ((0, 8),)),
        "value_bias": noise(keys[6], (D,), 0.2, 1.1953125, ((0, 8),)),
        "proj_weight": noise(keys[7], (D, D), (max(D // 16, 4)) ** -0.5, 0.75, ((0, 4), (1, 8))),
        "proj_bias": noise(keys[8], (D,), 0.5, 3.0, ((0, 8),)),
        "ln2_gain": jnp.clip(1.0 + 0.15 * jax.random.normal(keys[9], (D,), jnp.float32), 0.25, 1.75).astype(jnp.bfloat16),
        "ln2_bias": noise(keys[10], (D,), 0.5, 3.0, ((0, 8),)),
        "fc_weight": noise(keys[11], (D, FF), D ** -0.5, 0.1875, ((0, 8), (1, 4))),
        "fc_bias": noise(keys[12], (FF,), 0.5, 3.0, ((0, 8),)),
        "out_weight": noise(keys[13], (FF, D), FF ** -0.5, 0.09375, ((0, 4), (1, 8))),
        "out_bias": noise(keys[14], (D,), 0.5, 3.0, ((0, 8),)),
        "cotangent": heavy_noise(keys[15], (SEQS, SEQ_LEN, D), 1.0, 6.0, ((0, 8), (1, 4)), (0, 2, 8, 2.0)),
    }


NORM_EPS = 1e-05
GELU_ROOT = math.sqrt(2.0 / math.pi)
GELU_CUBE = 0.044715
MASK_VALUE = -1e+30

def norm_forward(residual):
    row_mean = lax.optimization_barrier(jnp.mean(residual, axis=-1, keepdims=True))
    centered = residual - row_mean
    row_var = lax.optimization_barrier(jnp.mean(centered * centered, axis=-1, keepdims=True))
    inv_std = lax.rsqrt(row_var + NORM_EPS)
    return (centered * inv_std, inv_std)

def norm_backward(grad_in, normed, inv_std, gain):
    scaled = grad_in * gain
    mean_scaled = lax.optimization_barrier(jnp.mean(scaled, axis=-1, keepdims=True))
    mean_cross = lax.optimization_barrier(jnp.mean(scaled * normed, axis=-1, keepdims=True))
    return inv_std * (scaled - mean_scaled - normed * mean_cross)

def gelu_pair(pre_act):
    inner_arg = GELU_ROOT * (pre_act + GELU_CUBE * pre_act * pre_act * pre_act)
    tangent = jnp.tanh(inner_arg)
    activated = 0.5 * pre_act * (1.0 + tangent)
    gelu_slope = 0.5 * (1.0 + tangent) + 0.5 * pre_act * (1.0 - tangent * tangent) * GELU_ROOT * (1.0 + 3.0 * GELU_CUBE * pre_act * pre_act)
    return (activated, gelu_slope)

def reference(block_input, segment_ids, ln1_gain, ln1_bias, qkv_weight, query_bias, value_bias, proj_weight, proj_bias, ln2_gain, ln2_bias, fc_weight, fc_bias, out_weight, out_bias, cotangent):
    qkv_flat = qkv_weight.reshape(D, 3 * D)
    gain_first = ln1_gain.astype(jnp.float32)
    shift_first = ln1_bias.astype(jnp.float32)
    query_shift = query_bias.astype(jnp.float32)
    value_shift = value_bias.astype(jnp.float32)
    proj_shift = proj_bias.astype(jnp.float32)
    gain_second = ln2_gain.astype(jnp.float32)
    shift_second = ln2_bias.astype(jnp.float32)
    fc_shift = fc_bias.astype(jnp.float32)
    out_shift = out_bias.astype(jnp.float32)
    positions = jnp.arange(SEQ_LEN, dtype=jnp.int32)
    score_scale = HD ** (-0.5)

    def one_sequence(totals, inputs):
        tokens, seg_row, grad_rows = inputs
        allowed = (positions[:, None] >= positions[None, :]) & (seg_row[:, None] == seg_row[None, :])
        resid_in = tokens.astype(jnp.float32)
        normed_one, inv_one = norm_forward(resid_in)
        hidden_one = (normed_one * gain_first + shift_first).astype(jnp.bfloat16)
        qkv_out = jnp.dot(hidden_one, qkv_flat, preferred_element_type=jnp.float32)
        queries = (qkv_out[:, :D] + query_shift).astype(jnp.bfloat16)
        keys_all = qkv_out[:, D:2 * D].astype(jnp.bfloat16)
        values_all = (qkv_out[:, 2 * D:] + value_shift).astype(jnp.bfloat16)
        query_heads = queries.astype(jnp.float32).reshape(SEQ_LEN, HEADS, HD)
        key_heads = keys_all.astype(jnp.float32).reshape(SEQ_LEN, HEADS, HD)
        value_heads = values_all.astype(jnp.float32).reshape(SEQ_LEN, HEADS, HD)
        raw_scores = jnp.einsum('qhd,khd->hqk', query_heads, key_heads) * score_scale
        scores = jnp.where(allowed[None], raw_scores, MASK_VALUE)
        top_score = lax.optimization_barrier(jnp.max(scores, axis=-1, keepdims=True))
        log_total = top_score + jnp.log(lax.optimization_barrier(jnp.sum(jnp.exp(scores - top_score), axis=-1, keepdims=True)))
        attn_probs = jnp.where(allowed[None], jnp.exp(scores - log_total), 0.0)
        probs_half = attn_probs.astype(jnp.bfloat16)
        attended = jnp.einsum('hqk,khd->qhd', probs_half.astype(jnp.float32), value_heads).reshape(SEQ_LEN, D).astype(jnp.bfloat16)
        resid_mid = resid_in + jnp.dot(attended, proj_weight, preferred_element_type=jnp.float32) + proj_shift
        normed_two, inv_two = norm_forward(resid_mid)
        hidden_two = (normed_two * gain_second + shift_second).astype(jnp.bfloat16)
        pre_act = jnp.dot(hidden_two, fc_weight, preferred_element_type=jnp.float32) + fc_shift
        activated, gelu_slope = gelu_pair(pre_act)
        activated = activated.astype(jnp.bfloat16)
        block_output = (resid_mid + jnp.dot(activated, out_weight, preferred_element_type=jnp.float32) + out_shift).astype(jnp.bfloat16)
        grad_out = grad_rows.astype(jnp.float32)
        out_shift_grad = lax.optimization_barrier(jnp.sum(grad_out, axis=0))
        out_weight_grad = jnp.dot(activated.T, grad_rows, preferred_element_type=jnp.float32)
        pre_grad = jnp.dot(grad_rows, out_weight.T, preferred_element_type=jnp.float32) * gelu_slope
        fc_shift_grad = lax.optimization_barrier(jnp.sum(pre_grad, axis=0))
        pre_grad_half = pre_grad.astype(jnp.bfloat16)
        fc_weight_grad = jnp.dot(hidden_two.T, pre_grad_half, preferred_element_type=jnp.float32)
        hidden_two_grad = jnp.dot(pre_grad_half, fc_weight.T, preferred_element_type=jnp.float32)
        gain_second_grad = lax.optimization_barrier(jnp.sum(hidden_two_grad * normed_two, axis=0))
        shift_second_grad = lax.optimization_barrier(jnp.sum(hidden_two_grad, axis=0))
        mid_grad = grad_out + norm_backward(hidden_two_grad, normed_two, inv_two, gain_second)
        proj_shift_grad = lax.optimization_barrier(jnp.sum(mid_grad, axis=0))
        mid_grad_half = mid_grad.astype(jnp.bfloat16)
        proj_weight_grad = jnp.dot(attended.T, mid_grad_half, preferred_element_type=jnp.float32)
        attended_grad = jnp.dot(mid_grad_half, proj_weight.T, preferred_element_type=jnp.float32).astype(jnp.bfloat16)
        grad_heads = attended_grad.astype(jnp.float32).reshape(SEQ_LEN, HEADS, HD)
        prob_grad = jnp.einsum('qhd,khd->hqk', grad_heads, value_heads)
        value_grad = jnp.einsum('hqk,qhd->khd', probs_half.astype(jnp.float32), grad_heads).reshape(SEQ_LEN, D)
        delta_rows = lax.optimization_barrier(jnp.sum(attn_probs * prob_grad, axis=-1, keepdims=True))
        score_grad = (attn_probs * (prob_grad - delta_rows) * score_scale).astype(jnp.bfloat16).astype(jnp.float32)
        query_grad = jnp.einsum('hqk,khd->qhd', score_grad, key_heads).reshape(SEQ_LEN, D)
        key_grad = jnp.einsum('hqk,qhd->khd', score_grad, query_heads).reshape(SEQ_LEN, D)
        query_shift_grad = lax.optimization_barrier(jnp.sum(query_grad, axis=0))
        value_shift_grad = lax.optimization_barrier(jnp.sum(value_grad, axis=0))
        qkv_grad = jnp.concatenate([query_grad, key_grad, value_grad], axis=1).astype(jnp.bfloat16)
        qkv_weight_grad = jnp.dot(hidden_one.T, qkv_grad, preferred_element_type=jnp.float32)
        hidden_one_grad = jnp.dot(qkv_grad, qkv_flat.T, preferred_element_type=jnp.float32)
        gain_first_grad = lax.optimization_barrier(jnp.sum(hidden_one_grad * normed_one, axis=0))
        shift_first_grad = lax.optimization_barrier(jnp.sum(hidden_one_grad, axis=0))
        input_grad = mid_grad + norm_backward(hidden_one_grad, normed_one, inv_one, gain_first)
        terms = (gain_first_grad, shift_first_grad, qkv_weight_grad, query_shift_grad, value_shift_grad, proj_weight_grad, proj_shift_grad, gain_second_grad, shift_second_grad, fc_weight_grad, fc_shift_grad, out_weight_grad, out_shift_grad)
        new_totals = tuple((total + term for total, term in zip(totals, terms)))
        return (new_totals, (block_output, input_grad))
    zero_init = (jnp.zeros((D,), jnp.float32), jnp.zeros((D,), jnp.float32), jnp.zeros((D, 3 * D), jnp.float32), jnp.zeros((D,), jnp.float32), jnp.zeros((D,), jnp.float32), jnp.zeros((D, D), jnp.float32), jnp.zeros((D,), jnp.float32), jnp.zeros((D,), jnp.float32), jnp.zeros((D,), jnp.float32), jnp.zeros((D, FF), jnp.float32), jnp.zeros((FF,), jnp.float32), jnp.zeros((FF, D), jnp.float32), jnp.zeros((D,), jnp.float32))
    totals, outputs = lax.scan(one_sequence, zero_init, (block_input, segment_ids, cotangent))
    block_output, input_grad = outputs
    return (block_output, input_grad, totals[0], totals[1], totals[2].reshape(D, 3, D), totals[3], totals[4], totals[5], totals[6], totals[7], totals[8], totals[9], totals[10], totals[11], totals[12])
```

```python
import jax
import jax.numpy as jnp
from jax import lax
from jax.sharding import PartitionSpec as P

D = 1024
HD = 64
FF = 4096


NORM_EPS = 1e-05
GELU_ROOT = 0.7978845608028654
GELU_CUBE = 0.044715
MASK_VALUE = -1e30


def norm_forward(residual):
    row_mean = jnp.mean(residual, axis=-1, keepdims=True)
    centered = residual - row_mean
    row_var = jnp.mean(centered * centered, axis=-1, keepdims=True)
    inv_std = lax.rsqrt(row_var + NORM_EPS)
    return (centered * inv_std, inv_std)


def norm_backward(grad_in, normed, inv_std, gain):
    scaled = grad_in * gain
    mean_scaled = jnp.mean(scaled, axis=-1, keepdims=True)
    mean_cross = jnp.mean(scaled * normed, axis=-1, keepdims=True)
    return inv_std * (scaled - mean_scaled - normed * mean_cross)


def gelu_pair(pre_act):
    inner_arg = GELU_ROOT * (pre_act + GELU_CUBE * pre_act * pre_act * pre_act)
    tangent = jnp.tanh(inner_arg)
    activated = 0.5 * pre_act * (1.0 + tangent)
    gelu_slope = 0.5 * (1.0 + tangent) + 0.5 * pre_act * (1.0 - tangent * tangent) * GELU_ROOT * (
        1.0 + 3.0 * GELU_CUBE * pre_act * pre_act
    )
    return (activated, gelu_slope)


def masked_scores(query_heads, key_heads, allowed):
    raw_scores = jnp.einsum(
        "qhd,khd->hqk", query_heads, key_heads, preferred_element_type=jnp.float32
    ) * HD ** (-0.5)
    return jnp.where(allowed[None], raw_scores, MASK_VALUE)


def attend(query_heads, key_heads, value_heads, allowed):
    scores = masked_scores(query_heads, key_heads, allowed)
    top_score = jnp.max(scores, axis=-1, keepdims=True)
    log_total = top_score + jnp.log(jnp.sum(jnp.exp(scores - top_score), axis=-1, keepdims=True))
    attn_probs = jnp.where(allowed[None], jnp.exp(scores - log_total), 0.0)
    probs_half = attn_probs.astype(jnp.bfloat16)
    attended = jnp.einsum(
        "hqk,khd->qhd", probs_half, value_heads, preferred_element_type=jnp.float32
    )
    return (attended.reshape(query_heads.shape[0], -1).astype(jnp.bfloat16), log_total)


def attend_back(query_heads, key_heads, value_heads, allowed, log_total, grad_heads):
    scores = masked_scores(query_heads, key_heads, allowed)
    attn_probs = jnp.where(allowed[None], jnp.exp(scores - log_total), 0.0)
    probs_half = attn_probs.astype(jnp.bfloat16)
    prob_grad = jnp.einsum(
        "qhd,khd->hqk", grad_heads, value_heads, preferred_element_type=jnp.float32
    )
    value_part = jnp.einsum(
        "hqk,qhd->khd", probs_half, grad_heads, preferred_element_type=jnp.float32
    )
    delta_rows = jnp.sum(attn_probs * prob_grad, axis=-1, keepdims=True)
    score_grad = (attn_probs * (prob_grad - delta_rows) * HD ** (-0.5)).astype(jnp.bfloat16)
    query_grad = jnp.einsum(
        "hqk,khd->qhd", score_grad, key_heads, preferred_element_type=jnp.float32
    )
    key_part = jnp.einsum(
        "hqk,qhd->khd", score_grad, query_heads, preferred_element_type=jnp.float32
    )
    key_count = key_heads.shape[0]
    return (
        query_grad.reshape(query_heads.shape[0], -1),
        key_part.reshape(key_count, -1),
        value_part.reshape(key_count, -1),
    )


def place_part(part, whole_len, start):
    return lax.dynamic_update_slice_in_dim(jnp.zeros((whole_len,), jnp.float32), part, start, 0)


def body(
    block_input,
    segment_ids,
    ln1_gain,
    ln1_bias,
    qkv_weight,
    query_bias,
    value_bias,
    proj_weight,
    proj_bias,
    ln2_gain,
    ln2_bias,
    fc_weight,
    fc_bias,
    out_weight,
    out_bias,
    cotangent,
):
    tokens = block_input[0]
    seg_whole = segment_ids[0]
    grad_rows = cotangent[0]
    seq_length = seg_whole.shape[0]
    ctx_rank = lax.axis_index("ctx")
    key_pos = jnp.arange(seq_length, dtype=jnp.int32)
    resid_in = tokens.astype(jnp.float32)
    normed_one, inv_one = norm_forward(resid_in)
    grad_out = grad_rows.astype(jnp.float32)
    out_shift_grad = jnp.sum(grad_out, axis=0)
    vectors = lax.all_gather(
        jnp.concatenate(
            [ln1_gain, ln1_bias, query_bias, value_bias, proj_bias, ln2_gain, ln2_bias, out_bias, fc_bias]
        ),
        "dp",
        axis=0,
    )
    slice_len = ln1_gain.shape[0]
    dp_size = vectors.shape[0]
    ff_whole = fc_bias.shape[0] * dp_size

    def vector(at):
        return vectors[:, at * slice_len : (at + 1) * slice_len].astype(jnp.float32).reshape(-1)

    qkv_cols = lax.all_gather(qkv_weight, "dp", axis=0, tiled=True).reshape(D, -1)
    proj_rows = lax.all_gather(proj_weight, "dp", axis=1, tiled=True)
    fc_cols = lax.all_gather(fc_weight, "dp", axis=0, tiled=True)
    out_rows = lax.all_gather(out_weight, "dp", axis=1, tiled=True)
    quarter = proj_rows.shape[0]
    unit_part = fc_cols.shape[1]
    gain_first = vector(0)
    shift_first = vector(1)
    query_shift = lax.dynamic_slice_in_dim(vector(2), ctx_rank * quarter, quarter)
    value_shift = lax.dynamic_slice_in_dim(vector(3), ctx_rank * quarter, quarter)
    proj_shift = vector(4)
    gain_second = vector(5)
    shift_second = vector(6)
    out_shift = vector(7)
    fc_shift = lax.dynamic_slice_in_dim(
        vectors[:, 8 * slice_len :].astype(jnp.float32).reshape(-1), ctx_rank * unit_part, unit_part
    )
    local_heads = quarter // HD
    allowed = (key_pos[:, None] >= key_pos[None, :]) & (seg_whole[:, None] == seg_whole[None, :])
    hidden_one = (normed_one * gain_first + shift_first).astype(jnp.bfloat16)
    hidden_all, grad_all = (
        lax.all_gather(hidden_one, "ctx", axis=0, tiled=True),
        lax.all_gather(grad_rows, "ctx", axis=0, tiled=True),
    )
    qkv_out = jnp.dot(hidden_all, qkv_cols, preferred_element_type=jnp.float32)
    queries = (qkv_out[:, :quarter] + query_shift).astype(jnp.bfloat16)
    keys_here = qkv_out[:, quarter : 2 * quarter].astype(jnp.bfloat16)
    values_here = (qkv_out[:, 2 * quarter :] + value_shift).astype(jnp.bfloat16)
    query_heads = queries.reshape(seq_length, local_heads, HD)
    key_heads = keys_here.reshape(seq_length, local_heads, HD)
    value_heads = values_here.reshape(seq_length, local_heads, HD)
    attended, log_total = attend(query_heads, key_heads, value_heads, allowed)
    resid_mid = (
        resid_in
        + lax.psum_scatter(
            jnp.dot(attended, proj_rows, preferred_element_type=jnp.float32).astype(jnp.bfloat16),
            "ctx",
            scatter_dimension=0,
            tiled=True,
        ).astype(jnp.float32)
        + proj_shift
    )
    normed_two, inv_two = norm_forward(resid_mid)
    hidden_two = (normed_two * gain_second + shift_second).astype(jnp.bfloat16)
    hidden_two_all = lax.all_gather(hidden_two, "ctx", axis=0, tiled=True)
    pre_act = jnp.dot(hidden_two_all, fc_cols, preferred_element_type=jnp.float32) + fc_shift
    activated, gelu_slope = gelu_pair(pre_act)
    activated = activated.astype(jnp.bfloat16)
    block_output = (
        resid_mid
        + lax.psum_scatter(
            jnp.dot(activated, out_rows, preferred_element_type=jnp.float32).astype(jnp.bfloat16),
            "ctx",
            scatter_dimension=0,
            tiled=True,
        ).astype(jnp.float32)
        + out_shift
    ).astype(jnp.bfloat16)
    out_weight_grad = jnp.dot(activated.T, grad_all, preferred_element_type=jnp.float32)
    pre_grad = jnp.dot(grad_all, out_rows.T, preferred_element_type=jnp.float32) * gelu_slope
    fc_shift_grad = place_part(jnp.sum(pre_grad, axis=0), ff_whole, ctx_rank * unit_part)
    pre_grad_half = pre_grad.astype(jnp.bfloat16)
    fc_weight_grad = jnp.dot(hidden_two_all.T, pre_grad_half, preferred_element_type=jnp.float32)
    hidden_two_grad = lax.psum_scatter(
        jnp.dot(pre_grad_half, fc_cols.T, preferred_element_type=jnp.float32).astype(jnp.bfloat16),
        "ctx",
        scatter_dimension=0,
        tiled=True,
    ).astype(jnp.float32)
    gain_second_grad = jnp.sum(hidden_two_grad * normed_two, axis=0)
    shift_second_grad = jnp.sum(hidden_two_grad, axis=0)
    mid_grad = grad_out + norm_backward(hidden_two_grad, normed_two, inv_two, gain_second)
    proj_shift_grad = jnp.sum(mid_grad, axis=0)
    mid_grad_half = mid_grad.astype(jnp.bfloat16)
    mid_all = lax.all_gather(mid_grad_half, "ctx", axis=0, tiled=True)
    proj_weight_grad = jnp.dot(attended.T, mid_all, preferred_element_type=jnp.float32)
    attended_grad = jnp.dot(mid_all, proj_rows.T, preferred_element_type=jnp.float32).astype(
        jnp.bfloat16
    )
    grad_heads = attended_grad.reshape(seq_length, local_heads, HD)
    query_grad, key_grad, value_grad = attend_back(
        query_heads, key_heads, value_heads, allowed, log_total, grad_heads
    )
    query_shift_grad = place_part(jnp.sum(query_grad, axis=0), D, ctx_rank * quarter)
    value_shift_grad = place_part(jnp.sum(value_grad, axis=0), D, ctx_rank * quarter)
    qkv_grad = jnp.concatenate([query_grad, key_grad, value_grad], axis=1).astype(jnp.bfloat16)
    qkv_weight_grad = jnp.dot(hidden_all.T, qkv_grad, preferred_element_type=jnp.float32).reshape(
        D, 3, quarter
    )
    hidden_one_grad = lax.psum_scatter(
        jnp.dot(qkv_grad, qkv_cols.T, preferred_element_type=jnp.float32).astype(jnp.bfloat16),
        "ctx",
        scatter_dimension=0,
        tiled=True,
    ).astype(jnp.float32)
    gain_first_grad = jnp.sum(hidden_one_grad * normed_one, axis=0)
    shift_first_grad = jnp.sum(hidden_one_grad, axis=0)
    input_grad = mid_grad + norm_backward(hidden_one_grad, normed_one, inv_one, gain_first)
    half = jnp.bfloat16
    matrix_sums = (
        lax.psum_scatter(qkv_weight_grad.astype(half), "dp", scatter_dimension=0, tiled=True),
        lax.psum_scatter(proj_weight_grad.astype(half), "dp", scatter_dimension=1, tiled=True),
        lax.psum_scatter(fc_weight_grad.astype(half), "dp", scatter_dimension=0, tiled=True),
        lax.psum_scatter(out_weight_grad.astype(half), "dp", scatter_dimension=1, tiled=True),
    )
    matrix_sums = tuple(m.astype(jnp.float32) for m in matrix_sums)
    packed = jnp.concatenate(
        [
            v.reshape(dp_size, -1)
            for v in (
                gain_first_grad,
                shift_first_grad,
                query_shift_grad,
                value_shift_grad,
                proj_shift_grad,
                gain_second_grad,
                shift_second_grad,
                out_shift_grad,
                fc_shift_grad,
            )
        ],
        axis=1,
    )
    packed = lax.psum(packed, ("dp", "ctx"))
    mine = lax.dynamic_index_in_dim(packed, lax.axis_index("dp"), 0, keepdims=False)
    order = (0, 1, 2, 3, 4, 5, 6, 8, 7)
    pieces = [mine[i * slice_len : (i + 1) * slice_len] for i in range(8)] + [mine[8 * slice_len :]]
    vector_sums = tuple(pieces[i] for i in order)
    return (
        block_output[None],
        input_grad[None],
        vector_sums[0],
        vector_sums[1],
        matrix_sums[0],
        vector_sums[2],
        vector_sums[3],
        matrix_sums[1],
        vector_sums[4],
        vector_sums[5],
        vector_sums[6],
        matrix_sums[2],
        vector_sums[7],
        matrix_sums[3],
        vector_sums[8],
    )


def solution(mesh):
    return jax.shard_map(
        body,
        mesh=mesh,
        in_specs=(
            P("dp", "ctx", None),
            P("dp", None),
            P("dp"),
            P("dp"),
            P("dp", None, "ctx"),
            P("dp"),
            P("dp"),
            P("ctx", "dp"),
            P("dp"),
            P("dp"),
            P("dp"),
            P("dp", "ctx"),
            P("dp"),
            P("ctx", "dp"),
            P("dp"),
            P("dp", "ctx", None),
        ),
        out_specs=(
            P("dp", "ctx", None),
            P("dp", "ctx", None),
            P("dp"),
            P("dp"),
            P("dp", None, "ctx"),
            P("dp"),
            P("dp"),
            P("ctx", "dp"),
            P("dp"),
            P("dp"),
            P("dp"),
            P("dp", "ctx"),
            P("dp"),
            P("ctx", "dp"),
            P("dp"),
        ),
        check_vma=False,
    )
```
